32 devices in a mesh: groups: 2 (over x), rows: 16 (over z, y, core).
Axes of the slice: x: 2, y: 2, z: 4, core: 2. Of those that a mesh axis runs over, the one named last changes fastest.
Arguments:
- points: bfloat16 [64, 32768], P(None, ('groups', 'rows')), parts along dimension 1, may hold values from -12 to 12
- landmarks: bfloat16 [64, 2048], P(None, 'groups'), parts along dimension 1, may hold values from -12 to 12
- chol: float32 [2048, 1024], P('groups'), parts along dimension 0, as said below
- ridge: float32 [2], P('groups'), parts along dimension 0, may hold values from 0.5 to 2
- solution: float32 [8, 32768], P(None, ('groups', 'rows')), parts along dimension 1, may hold values from -6 to 6
- residual: float32 [8, 32768], P(None, ('groups', 'rows')), parts along dimension 1, may hold values from -6 to 6
- direction: float32 [8, 32768], P(None, ('groups', 'rows')), parts along dimension 1, may hold values from -6 to 6
- rz_prev: float32 [16], P('groups'), parts along dimension 0, may hold values from 8192 to 32768
Outputs:
- solution_new: float32 [8, 32768], P(None, ('groups', 'rows')), parts along dimension 1
- residual_new: float32 [8, 32768], P(None, ('groups', 'rows')), parts along dimension 1
- direction_new: float32 [8, 32768], P(None, ('groups', 'rows')), parts along dimension 1
- inner_new: float32 [16], P('groups'), parts along dimension 0
The draws below stay inside these ranges and needn't reach their ends.
There are 2 independent parts, one for each index of `groups`. The reference program is written for one: setup_inputs(seed, part) draws one part's arguments, and reference() takes and returns one part's arrays. A program takes and returns all parts, laid end to end along the dimension named above; each array names one. Nothing has to cross between parts.
Inputs may be any that keep to these rules, and one draw needn't show every extreme that they name: chol is lower triangular with a positive diagonal, and chol chol^T = ridge k(landmarks, landmarks) + cross^T cross, with k and cross as in the reference program.
All inputs are finite; a program needn't handle non-finite values.
Results may differ from the reference program's by a relative error of at most 0.0064.
Values may be sent and summed in bfloat16 or wider, within the bound.
A program may use at most 64 MiB of HBM per device.

```python
import math
import jax
import jax.numpy as jnp
from jax import lax

FEAT = 64
OUTS = 8
LAND = 1024
NPTS = 16384


latent_dims = 8


def shared_sample(key):
    base = jax.random.fold_in(key, 23)
    keys = jax.random.split(base, 6)
    basis = jnp.clip(jax.random.normal(keys[0], (FEAT, latent_dims), jnp.float32), -3.0, 3.0)
    spread = 0.5
    latent_points = jax.random.uniform(keys[1], (latent_dims, NPTS), jnp.float32, -1.5, 1.5)
    latent_marks = jax.random.uniform(keys[2], (latent_dims, LAND), jnp.float32, -1.5, 1.5)
    ridge_value = jnp.exp(jax.random.uniform(keys[5], (1,), jnp.float32, math.log(0.5), math.log(2.0)))
    noise_points = spread * jnp.clip(jax.random.normal(keys[3], (FEAT, NPTS), jnp.float32), -4.0, 4.0)
    noise_marks = spread * jnp.clip(jax.random.normal(keys[4], (FEAT, LAND), jnp.float32), -4.0, 4.0)
    points = jnp.clip(jnp.dot(basis, latent_points, precision=lax.Precision.HIGHEST) + noise_points, -12.0, 12.0)
    landmarks = jnp.clip(jnp.dot(basis, latent_marks, precision=lax.Precision.HIGHEST) + noise_marks, -12.0, 12.0)
    return (points, landmarks, ridge_value)


def square_sums(values):
    return jnp.sum(values * values, axis=0)


def gauss_kernel(left, right):
    inner = jnp.dot(left.T, right, precision=lax.Precision.HIGHEST)
    dist = square_sums(left)[:, None] + square_sums(right)[None, :] - 2.0 * inner
    return jnp.exp(-dist / (2.0 * FEAT))


def draw_points(key, part):
    return shared_sample(key)[0].astype(jnp.bfloat16)


def draw_landmarks(key, part):
    return shared_sample(key)[1].astype(jnp.bfloat16)


def draw_ridge(key, part):
    return shared_sample(key)[2].astype(jnp.float32)


def draw_chol(key, part):
    points, landmarks, ridge_value = shared_sample(key)
    rounded_points = points.astype(jnp.bfloat16).astype(jnp.float32)
    rounded_marks = landmarks.astype(jnp.bfloat16).astype(jnp.float32)
    cross = gauss_kernel(rounded_points, rounded_marks)
    inner = ridge_value[0] * gauss_kernel(rounded_marks, rounded_marks)
    inner = inner + jnp.dot(cross.T, cross, precision=lax.Precision.HIGHEST)
    inner = 0.5 * (inner + inner.T)
    return jnp.linalg.cholesky(inner).astype(jnp.float32)


def block_levels(rng, extent, cuts, smallest, top_value):
    loudness = 1.0
    for position, shards_of in cuts:
        draws = jax.random.uniform(jax.random.fold_in(jax.random.fold_in(rng, 6), position), (shards_of,), jnp.float32, smallest / len(cuts), top_value / len(cuts))
        loudness = loudness * jnp.repeat(jnp.exp(draws), extent[position] // shards_of).reshape((-1,) + (1,) * (len(extent) - 1 - position))
    return loudness


def gaussian(rng, dims, width, bound, shards=(), held_as=jnp.bfloat16):
    gain = block_levels(rng, dims, shards, -0.22, 0.18) if shards else 1.0
    values = jax.random.normal(rng, dims, jnp.float32) * width * gain
    return jnp.minimum(jnp.maximum(values, -bound), bound).astype(held_as)


def setup_inputs(seed: int = 0, part: int = 0) -> dict:
    splits = jax.random.split(jax.random.key(seed), 9)
    part_keys = jax.random.split(jax.random.fold_in(splits[8], part), 9)
    return {
        "points": draw_points(jax.random.fold_in(jax.random.fold_in(splits[8], part), 71), part),
        "landmarks": draw_landmarks(jax.random.fold_in(jax.random.fold_in(splits[8], part), 71), part),
        "chol": draw_chol(jax.random.fold_in(jax.random.fold_in(splits[8], part), 71), part),
        "ridge": draw_ridge(jax.random.fold_in(jax.random.fold_in(splits[8], part), 71), part),
        "solution": gaussian(part_keys[4], (OUTS, NPTS), 1.0, 6.0, ((1, 16),), jnp.float32),
        "residual": gaussian(part_keys[5], (OUTS, NPTS), 1.0, 6.0, ((1, 16),), jnp.float32),
        "direction": gaussian(part_keys[6], (OUTS, NPTS), 1.0, 6.0, ((1, 16),), jnp.float32),
        "rz_prev": jnp.clip(jnp.exp(jax.random.uniform(part_keys[7], (OUTS,), jnp.float32, math.log(8192.0), math.log(32768.0))), 8192.0, 32768.0),
    }


def square_norms(features):
    wide = features.astype(jnp.float32)
    return jnp.sum(wide * wide, axis=0)

def kernel_block(row_points, row_norms, col_points, col_norms):
    scale = 0.5 / row_points.shape[0]
    cross = lax.dot_general(row_points.astype(jnp.float32), col_points.astype(jnp.float32), (((0,), (0,)), ((), ())), preferred_element_type=jnp.float32)
    dist = row_norms[:, None] + col_norms[None, :] - 2.0 * cross
    return jnp.exp(-scale * dist)

def reference(points, landmarks, chol, ridge, solution, residual, direction, rz_prev):
    ridge_value = ridge[0]
    norms = square_norms(points)
    landmark_norms = square_norms(landmarks)
    landmark_kernel = kernel_block(points, norms, landmarks, landmark_norms)
    projection = jnp.dot(residual, landmark_kernel, precision=lax.Precision.HIGHEST)
    coeffs = jax.scipy.linalg.cho_solve((chol, True), projection.T)
    precond = (residual - jnp.dot(coeffs.T, landmark_kernel.T, precision=lax.Precision.HIGHEST)) / ridge_value
    inner_new = jnp.sum(precond * residual, axis=1)
    direction_new = precond + (inner_new / rz_prev)[:, None] * direction
    direction_low = direction_new.astype(jnp.bfloat16)
    total = points.shape[1]
    block_len = math.gcd(total, 512)
    blocks = total // block_len
    feature_count = points.shape[0]
    point_blocks = jnp.moveaxis(points.reshape(feature_count, blocks, block_len), 1, 0)
    norm_blocks = norms.reshape(blocks, block_len)

    def one_block(inputs):
        block_points, block_norms = inputs
        kernel_tile = kernel_block(block_points, block_norms, points, norms).astype(jnp.bfloat16)
        return lax.dot_general(direction_low.astype(jnp.float32), kernel_tile.astype(jnp.float32), (((1,), (1,)), ((), ())), preferred_element_type=jnp.float32)
    stacked = lax.map(one_block, (point_blocks, norm_blocks))
    kernel_part = jnp.moveaxis(stacked, 0, 1).reshape(direction_new.shape[0], total)
    image = kernel_part + ridge_value * direction_new
    curvature = jnp.sum(direction_new * image, axis=1)
    alpha = inner_new / curvature
    solution_new = solution + alpha[:, None] * direction_new
    residual_new = residual - alpha[:, None] * image
    return (solution_new, residual_new, direction_new, inner_new)
```

```python
import functools
import math

import jax
import jax.numpy as jnp
from jax import lax
from jax.experimental import pallas as pl
from jax.experimental.pallas import tpu as pltpu
from jax.sharding import PartitionSpec as P

HIGH = lax.Precision.HIGHEST
TILE = 128
CHUNK = 256
STORED_BLOCKS = 16


def dot_nn(left, right, precision=None):
    return lax.dot_general(
        left, right, (((1,), (0,)), ((), ())), precision=precision, preferred_element_type=jnp.float32
    )


def dot_nt(left, right, precision=None):
    return lax.dot_general(
        left, right, (((1,), (1,)), ((), ())), precision=precision, preferred_element_type=jnp.float32
    )


def dot_tn(left, right):
    return lax.dot_general(
        left, right, (((0,), (0,)), ((), ())), preferred_element_type=jnp.float32
    )


def norm_rows(features, first):
    wide = features.astype(jnp.float32)
    half = -0.5 * jnp.sum(wide * wide, axis=0, keepdims=True)
    top = half.astype(jnp.bfloat16).astype(jnp.float32)
    rest = half - top
    mid = rest.astype(jnp.bfloat16).astype(jnp.float32)
    low = rest - mid
    row = lax.broadcasted_iota(jnp.int32, (16, features.shape[1]), 0)
    at = 0 if first else 3
    ones = 3 - at
    rows = jnp.where((row >= ones) & (row < ones + 3), 1.0, 0.0)
    rows = jnp.where(row == at, top, rows)
    rows = jnp.where(row == at + 1, mid, rows)
    rows = jnp.where(row == at + 2, low, rows)
    return rows.astype(jnp.bfloat16)


def eye_mask(width):
    shape = (8, width)
    return lax.broadcasted_iota(jnp.int32, shape, 0) == lax.broadcasted_iota(jnp.int32, shape, 1)


def to_row(column, width):
    return jnp.sum(jnp.where(eye_mask(width), column, 0.0), axis=0, keepdims=True)


def to_column(row):
    return jnp.sum(jnp.where(eye_mask(row.shape[1]), row, 0.0), axis=1, keepdims=True)


def kernel(
    n,
    keep,
    points_ref,
    landmarks_ref,
    chol_hbm,
    ridge_ref,
    solution_ref,
    residual_ref,
    direction_ref,
    rz_ref,
    solution_out,
    residual_out,
    direction_out,
    inner_out,
    chol,
    inverse,
    points,
    own_aug,
    col_aug,
    cross_t,
    kernel_store,
    rs_send,
    rs_recv,
    ag,
    proj,
    work,
    inner_buf,
    dirs,
    curv_buf,
    chol_sem,
    rs_sems,
    ag_sems,
    inner_sems,
    dir_sems,
    curv_sems,
    point_recv,
    point_fwd,
    point_side,
    point_back,
):
    me = lax.axis_index("rows")
    feat, local = points_ref.shape
    land = landmarks_ref.shape[1]
    outs = residual_ref.shape[0]
    chips = n // 2
    half = chips // 2
    core = me % 2
    chip = me // 2
    odd = chip % 2
    pos = (1 - odd) * (chip // 2) + odd * (chips - (chip + 1) // 2)
    scale = math.log2(math.e) / feat

    def row_of(position, lane):
        position = (position + chips) % chips
        upper = position // half
        at = (1 - upper) * (2 * position) + upper * (2 * chips - 1 - 2 * position)
        return at * 2 + (core + lane) % 2

    def remote(src, dst, send, recv, to):
        return pltpu.make_async_remote_copy(
            src_ref=src,
            dst_ref=dst,
            send_sem=send,
            recv_sem=recv,
            device_id={"rows": to},
            device_id_type=pl.DeviceIdType.MESH,
        )

    def others(body):
        lax.fori_loop(1, n, lambda k, carry: (body((me + k) % n), carry)[1], 0)

    def send_all(src_of, buf, sems):
        others(lambda to: remote(src_of(to), buf.at[me], sems.at[0, to], sems.at[1, me], to).start())

    def wait_all(src_of, buf, sems):
        others(lambda to: remote(src_of(to), buf.at[to], sems.at[0, to], sems.at[1, to], to).wait_recv())

    def drain(src_of, buf, sems):
        others(lambda to: remote(src_of(to), buf.at[me], sems.at[0, to], sems.at[1, me], to).wait_send())

    chol_copy = pltpu.make_async_copy(chol_hbm, chol, chol_sem)
    chol_copy.start()

    barrier = pltpu.get_barrier_semaphore()
    others(lambda to: pl.semaphore_signal(
        barrier, inc=1, device_id={"rows": to}, device_id_type=pl.DeviceIdType.MESH))
    pl.semaphore_wait(barrier, n - 1)

    right = row_of(pos + 1, 0)
    left = row_of(pos - 1, 0)
    partner = row_of(pos, 1)
    own_slot = points.at[me]
    first_right = remote(points_ref, own_slot, point_fwd.at[me], point_recv.at[me], right)
    first_left = remote(points_ref, own_slot, point_back, point_recv.at[me], left)
    first_side = remote(points_ref, own_slot, point_side.at[me], point_recv.at[me], partner)
    first_right.start()
    first_left.start()
    first_side.start()

    own_aug[0:feat, :] = points_ref[...]
    own_aug[feat:, :] = norm_rows(points_ref[...], True)
    col_aug[0:feat, :] = landmarks_ref[...]
    col_aug[feat:, :] = norm_rows(landmarks_ref[...], False)

    def entries(left_aug, at, right_aug):
        return jnp.exp2(dot_tn(left_aug[:, pl.ds(at, CHUNK)], right_aug[...]) * scale)

    proj[...] = jnp.zeros_like(proj)

    def project(i, carry):
        at = pl.multiple_of(i * CHUNK, CHUNK)
        proj[...] += dot_nn(residual_ref[:, pl.ds(at, CHUNK)], entries(own_aug, at, col_aug), HIGH)
        return carry

    lax.fori_loop(0, local // CHUNK, project, 0)

    tiles = land // TILE
    rows_per = outs * tiles // n
    for piece in range(n):
        h, j = piece // tiles, piece % tiles
        rs_send[piece] = proj[h * rows_per:(h + 1) * rows_per, j * TILE:(j + 1) * TILE]
    send_all(lambda to: rs_send.at[to], rs_recv, rs_sems)
    rs_recv[me] = rs_send[me]

    def landmark_rows(i, carry):
        at = pl.multiple_of(i * CHUNK, CHUNK)
        cross_t[pl.ds(at, CHUNK), :] = entries(col_aug, at, own_aug)
        return carry

    lax.fori_loop(0, land // CHUNK, landmark_rows, 0)

    def make_block(owner, slot):
        col_aug[0:feat, :] = points[owner]
        col_aug[feat:, :] = norm_rows(points[owner], False)

        def step(i, carry):
            at = pl.multiple_of(i * CHUNK, CHUNK)
            kernel_store[slot, pl.ds(at, CHUNK), :] = entries(col_aug, at, own_aug).astype(jnp.bfloat16)
            return carry

        lax.fori_loop(0, local // CHUNK, step, 0)

    own_points = pltpu.make_async_copy(points_ref, own_slot, chol_sem)
    chol_copy.wait()
    own_points.start()
    own_points.wait()

    row = lax.broadcasted_iota(jnp.int32, (TILE, TILE), 0)
    col = lax.broadcasted_iota(jnp.int32, (TILE, TILE), 1)

    blocks = [chol[b * TILE:(b + 1) * TILE, b * TILE:(b + 1) * TILE] for b in range(tiles)]
    for b in range(tiles):
        inverse[b] = jnp.where(row == col, 1.0 / blocks[b], 0.0)
    size = 1
    while size < TILE:
        below = (row // size == col // size + 1) & (row // (2 * size) == col // (2 * size))
        for b in range(tiles):
            off = jnp.where(below, chol[b * TILE:(b + 1) * TILE, b * TILE:(b + 1) * TILE], 0.0)
            if size == 1:
                on_row = jnp.sum(inverse[b], axis=1, keepdims=True)
                on_col = jnp.sum(inverse[b], axis=0, keepdims=True)
                change = on_row * off * on_col
            else:
                change = dot_nn(dot_nn(inverse[b], off, HIGH), inverse[b], HIGH)
            inverse[b] = inverse[b] - change
        size *= 2

    wait_all(lambda to: rs_send.at[to], rs_recv, rs_sems)
    ag[me] = jnp.sum(rs_recv[...], axis=0)
    send_all(lambda to: ag.at[me], ag, ag_sems)

    if keep:
        make_block(me, me)

    def relay(s, both):
        near = row_of(pos - s, 0)
        remote(points_ref, points.at[near], point_fwd.at[near], point_recv.at[near], right).wait_recv()
        if both:
            remote(points.at[near], points.at[near], point_fwd.at[near], point_recv.at[near], right).start()
        remote(points.at[near], points.at[near], point_side.at[near], point_recv.at[near], partner).start()
        if both:
            far = row_of(pos + s, 0)
            remote(points_ref, points.at[far], point_fwd.at[far], point_recv.at[far], left).wait_recv()
            remote(points.at[far], points.at[far], point_side.at[far], point_recv.at[far], partner).start()

            @pl.when(s < half - 1)
            def _():
                remote(points.at[far], points.at[far], point_fwd.at[far], point_recv.at[far], left).start()

        def build(lane):
            def one(way, carry):
                owner = row_of(pos - s + 2 * s * way, lane)
                if lane == 1:
                    remote(points_ref, points.at[owner], point_side.at[owner], point_recv.at[owner], partner).wait_recv()
                if keep:
                    make_block(owner, owner)
                return carry

            lax.fori_loop(0, 2 if both else 1, one, 0)

        build(0)
        build(1)

    relay(1, True)
    remote(points_ref, points.at[partner], point_side.at[partner], point_recv.at[partner], partner).wait_recv()

    wait_all(lambda to: ag.at[me], ag, ag_sems)
    for piece in range(n):
        h, j = piece // tiles, piece % tiles
        work[h * rows_per:(h + 1) * rows_per, j * TILE:(j + 1) * TILE] = ag[piece]
    for b in range(tiles):
        at, end = b * TILE, (b + 1) * TILE
        solved = dot_nt(work[:, at:end], inverse[b], HIGH)
        work[:, at:end] = solved
        if end < land:
            work[:, end:] -= dot_nt(solved, chol[end:, at:end], HIGH)
    for b in reversed(range(tiles)):
        at, end = b * TILE, (b + 1) * TILE
        solved = dot_nn(work[:, at:end], inverse[b], HIGH)
        work[:, at:end] = solved
        if at > 0:
            work[:, :at] -= dot_nn(solved, chol[at:end, :at], HIGH)

    ridge = ridge_ref[0]
    residual = residual_ref[...]
    precond = (residual - dot_nn(work[...], cross_t[...], HIGH)) / ridge
    inner_buf[me] = to_row(jnp.sum(precond * residual, axis=1, keepdims=True), TILE)
    send_all(lambda to: inner_buf.at[me], inner_buf, inner_sems)

    if keep:
        make_block(partner, partner)
    lax.fori_loop(2, min(3, half), lambda s, carry: (relay(s, True), carry)[1], 0)
    wait_all(lambda to: inner_buf.at[me], inner_buf, inner_sems)
    inner_row = jnp.sum(inner_buf[...], axis=0)
    inner_out[...] = inner_row[:, :outs]
    inner = to_column(inner_row)
    direction_new = precond + (inner / to_column(rz_ref[...])) * direction_ref[...]
    direction_out[...] = direction_new
    dirs[me] = direction_new.astype(jnp.bfloat16)
    send_all(lambda to: dirs.at[me], dirs, dir_sems)

    lax.fori_loop(3, half, lambda s, carry: (relay(s, True), carry)[1], 0)
    relay(half, False)

    def image_part(owner, slot):
        if not keep:
            make_block(owner, slot)
        proj[...] += dot_nn(dirs[owner], kernel_store[slot])

    proj[...] = jnp.zeros_like(proj)
    image_part(me, me if keep else 0)

    def gather_image(to):
        remote(dirs.at[me], dirs.at[to], dir_sems.at[0, to], dir_sems.at[1, to], to).wait_recv()
        image_part(to, to if keep else 0)

    others(gather_image)

    direction_new = direction_out[...]
    image = proj[...] + ridge * direction_new
    curv_buf[me] = to_row(jnp.sum(direction_new * image, axis=1, keepdims=True), TILE)
    send_all(lambda to: curv_buf.at[me], curv_buf, curv_sems)

    drain(lambda to: rs_send.at[to], rs_recv, rs_sems)
    drain(lambda to: ag.at[me], ag, ag_sems)
    drain(lambda to: inner_buf.at[me], inner_buf, inner_sems)
    drain(lambda to: dirs.at[me], dirs, dir_sems)
    first_right.wait_send()
    first_left.wait_send()
    first_side.wait_send()

    def relay_drain(s, both):
        near = row_of(pos - s, 0)
        remote(points.at[near], points.at[near], point_side.at[near], point_recv.at[near], partner).wait_send()
        if both:
            remote(points.at[near], points.at[near], point_fwd.at[near], point_recv.at[near], right).wait_send()
            far = row_of(pos + s, 0)
            remote(points.at[far], points.at[far], point_side.at[far], point_recv.at[far], partner).wait_send()

            @pl.when(s < half - 1)
            def _():
                remote(points.at[far], points.at[far], point_fwd.at[far], point_recv.at[far], left).wait_send()

    lax.fori_loop(1, half, lambda s, carry: (relay_drain(s, True), carry)[1], 0)
    relay_drain(half, False)

    wait_all(lambda to: curv_buf.at[me], curv_buf, curv_sems)
    alpha = to_column(inner_out[...] / jnp.sum(curv_buf[...], axis=0)[:, :outs])
    solution_out[...] = solution_ref[...] + alpha * direction_new
    residual_out[...] = residual_ref[...] - alpha * image
    drain(lambda to: curv_buf.at[me], curv_buf, curv_sems)


def solution(mesh):
    n = mesh.shape["rows"]

    def local(points, landmarks, chol, ridge, solution, residual, direction, rz_prev):
        feat, own = points.shape
        land = landmarks.shape[1]
        outs = residual.shape[0]
        keep = n <= STORED_BLOCKS
        piece = outs * land // (TILE * n)
        f32, bf16 = jnp.float32, jnp.bfloat16
        vmem = pl.BlockSpec(memory_space=pltpu.VMEM)
        wide = jax.ShapeDtypeStruct((outs, own), f32)
        dma = pltpu.SemaphoreType.DMA
        results = pl.pallas_call(
            functools.partial(kernel, n, keep),
            out_shape=(wide, wide, wide, jax.ShapeDtypeStruct((1, outs), f32)),
            in_specs=[
                vmem,
                vmem,
                pl.BlockSpec(memory_space=pl.ANY),
                pl.BlockSpec(memory_space=pltpu.SMEM),
                vmem,
                vmem,
                vmem,
                vmem,
            ],
            out_specs=(vmem,) * 4,
            scratch_shapes=[
                pltpu.VMEM((land, land), f32),
                pltpu.VMEM((land // TILE, TILE, TILE), f32),
                pltpu.VMEM((n, feat, own), bf16),
                pltpu.VMEM((feat + 16, own), bf16),
                pltpu.VMEM((feat + 16, own), bf16),
                pltpu.VMEM((land, own), f32),
                pltpu.VMEM((n if keep else 1, own, own), bf16),
                pltpu.VMEM((n, piece, TILE), f32),
                pltpu.VMEM((n, piece, TILE), f32),
                pltpu.VMEM((n, piece, TILE), f32),
                pltpu.VMEM((outs, land), f32),
                pltpu.VMEM((outs, land), f32),
                pltpu.VMEM((n, 1, TILE), f32),
                pltpu.VMEM((n, outs, own), bf16),
                pltpu.VMEM((n, 1, TILE), f32),
                dma,
                dma((2, n)),
                dma((2, n)),
                dma((2, n)),
                dma((2, n)),
                dma((2, n)),
                dma((n,)),
                dma((n,)),
                dma((n,)),
                dma,
            ],
            compiler_params=pltpu.CompilerParams(
                collective_id=0, has_side_effects=True, vmem_limit_bytes=62 * 1024 * 1024
            ),
            name="cg_step",
        )(points, landmarks, chol, ridge, solution, residual, direction, rz_prev.reshape(1, outs))
        return (results[0], results[1], results[2], results[3].reshape(outs))

    wide_spec = P(None, ("groups", "rows"))
    in_specs = (
        wide_spec,
        P(None, "groups"),
        P("groups", None),
        P("groups"),
        wide_spec,
        wide_spec,
        wide_spec,
        P("groups"),
    )
    out_specs = (wide_spec, wide_spec, wide_spec, P("groups"))
    return jax.shard_map(local, mesh=mesh, in_specs=in_specs, out_specs=out_specs, check_vma=False)
```

```python
import functools
import math

import jax
import jax.numpy as jnp
from jax import lax
from jax.experimental import pallas as pl
from jax.experimental.pallas import tpu as pltpu
from jax.sharding import PartitionSpec as P

HIGH = lax.Precision.HIGHEST
TILE = 128
CHUNK = 256
GROUP = 2 * TILE
STORED_BLOCKS = 16


def dot_nn(left, right, precision=None):
    return lax.dot_general(
        left, right, (((1,), (0,)), ((), ())), precision=precision, preferred_element_type=jnp.float32
    )


def dot_nt(left, right, precision=None):
    return lax.dot_general(
        left, right, (((1,), (1,)), ((), ())), precision=precision, preferred_element_type=jnp.float32
    )


def dot_tn(left, right):
    return lax.dot_general(
        left, right, (((0,), (0,)), ((), ())), preferred_element_type=jnp.float32
    )


def split(values):
    top = values.astype(jnp.bfloat16).astype(jnp.float32)
    rest = values - top
    mid = rest.astype(jnp.bfloat16).astype(jnp.float32)
    return top, mid, rest - mid


def store_split(ref, at, values):
    for term, part in enumerate(split(values)):
        ref[(term,) + at] = part.astype(jnp.bfloat16)


def dot_split(left, parts, dot):
    outs = left.shape[0]
    stacked = jnp.concatenate(split(left), axis=0).astype(jnp.bfloat16)
    high = dot(stacked, parts[0])
    mid = dot(stacked[:2 * outs], parts[1])
    low = dot(stacked[:2 * outs], parts[2])
    small = low[:outs] + mid[outs:] + high[2 * outs:]
    return high[:outs] + (high[outs:2 * outs] + mid[:outs] + small)


def norm_rows(features, first):
    wide = features.astype(jnp.float32)
    half = -0.5 * jnp.sum(wide * wide, axis=0, keepdims=True)
    top = half.astype(jnp.bfloat16).astype(jnp.float32)
    rest = half - top
    mid = rest.astype(jnp.bfloat16).astype(jnp.float32)
    low = rest - mid
    row = lax.broadcasted_iota(jnp.int32, (16, features.shape[1]), 0)
    at = 0 if first else 3
    ones = 3 - at
    rows = jnp.where((row >= ones) & (row < ones + 3), 1.0, 0.0)
    rows = jnp.where(row == at, top, rows)
    rows = jnp.where(row == at + 1, mid, rows)
    rows = jnp.where(row == at + 2, low, rows)
    return rows.astype(jnp.bfloat16)


def eye_mask(width):
    shape = (8, width)
    return lax.broadcasted_iota(jnp.int32, shape, 0) == lax.broadcasted_iota(jnp.int32, shape, 1)


def to_row(column, width):
    return jnp.sum(jnp.where(eye_mask(width), column, 0.0), axis=0, keepdims=True)


def to_column(row):
    return jnp.sum(jnp.where(eye_mask(row.shape[1]), row, 0.0), axis=1, keepdims=True)


def kernel(
    n,
    keep,
    points_ref,
    landmarks_ref,
    chol_hbm,
    ridge_ref,
    residual_ref,
    direction_ref,
    rz_ref,
    image_out,
    direction_out,
    inner_out,
    alpha_out,
    chol,
    chol_parts,
    inverse_parts,
    inverse,
    points,
    own_aug,
    col_aug,
    cross_t,
    kernel_store,
    rs_send,
    rs_recv,
    ag,
    proj,
    work,
    inner_buf,
    dirs,
    curv_buf,
    chol_sem,
    rs_sems,
    ag_sems,
    inner_sems,
    dir_sems,
    curv_sems,
    point_recv,
    point_fwd,
    point_side,
    point_back,
):
    me = lax.axis_index("rows")
    feat, local = points_ref.shape
    land = landmarks_ref.shape[1]
    outs = residual_ref.shape[0]
    chips = n // 2
    half = chips // 2
    core = me % 2
    chip = me // 2
    odd = chip % 2
    pos = (1 - odd) * (chip // 2) + odd * (chips - (chip + 1) // 2)
    scale = math.log2(math.e) / feat

    def row_of(position, lane):
        position = (position + chips) % chips
        upper = position // half
        at = (1 - upper) * (2 * position) + upper * (2 * chips - 1 - 2 * position)
        return at * 2 + (core + lane) % 2

    def remote(src, dst, send, recv, to):
        return pltpu.make_async_remote_copy(
            src_ref=src,
            dst_ref=dst,
            send_sem=send,
            recv_sem=recv,
            device_id={"rows": to},
            device_id_type=pl.DeviceIdType.MESH,
        )

    def others(body):
        lax.fori_loop(1, n, lambda k, carry: (body((me + k) % n), carry)[1], 0)

    def send_all(src_of, buf, sems):
        others(lambda to: remote(src_of(to), buf.at[me], sems.at[0, to], sems.at[1, me], to).start())

    def wait_all(src_of, buf, sems):
        others(lambda to: remote(src_of(to), buf.at[to], sems.at[0, to], sems.at[1, to], to).wait_recv())

    def drain(src_of, buf, sems):
        others(lambda to: remote(src_of(to), buf.at[me], sems.at[0, to], sems.at[1, me], to).wait_send())

    chol_copy = pltpu.make_async_copy(chol_hbm, chol, chol_sem)
    chol_copy.start()

    barrier = pltpu.get_barrier_semaphore()
    others(lambda to: pl.semaphore_signal(
        barrier, inc=1, device_id={"rows": to}, device_id_type=pl.DeviceIdType.MESH))

    right = row_of(pos + 1, 0)
    left = row_of(pos - 1, 0)
    partner = row_of(pos, 1)
    own_slot = points.at[me]
    first_right = remote(points_ref, own_slot, point_fwd.at[me], point_recv.at[me], right)
    first_left = remote(points_ref, own_slot, point_back, point_recv.at[me], left)
    first_side = remote(points_ref, own_slot, point_side.at[me], point_recv.at[me], partner)

    own_aug[0:feat, :] = points_ref[...]
    own_aug[feat:, :] = norm_rows(points_ref[...], True)
    col_aug[0:feat, :] = landmarks_ref[...]
    col_aug[feat:, :] = norm_rows(landmarks_ref[...], False)

    def entries(left_aug, at, right_aug):
        return jnp.exp2(dot_tn(left_aug[:, pl.ds(at, CHUNK)], right_aug[...]) * scale)

    proj[...] = jnp.zeros_like(proj)

    def project(i, carry):
        at = pl.multiple_of(i * CHUNK, CHUNK)
        parts = [part.astype(jnp.bfloat16) for part in split(entries(own_aug, at, col_aug))]
        proj[...] += dot_split(residual_ref[:, pl.ds(at, CHUNK)], parts, dot_nn)
        return carry

    lax.fori_loop(0, local // CHUNK, project, 0)

    pl.semaphore_wait(barrier, n - 1)

    tiles = land // TILE
    groups = land // GROUP
    rows_per = outs * tiles // n
    for piece in range(n):
        h, j = piece // tiles, piece % tiles
        rs_send[piece] = proj[h * rows_per:(h + 1) * rows_per, j * TILE:(j + 1) * TILE]
    send_all(lambda to: rs_send.at[to], rs_recv, rs_sems)
    rs_recv[me] = rs_send[me]
    first_right.start()
    first_left.start()
    first_side.start()

    def landmark_rows(i, carry):
        at = pl.multiple_of(i * CHUNK, CHUNK)
        store_split(cross_t, (pl.ds(at, CHUNK), slice(None)), entries(col_aug, at, own_aug))
        return carry

    lax.fori_loop(0, land // CHUNK, landmark_rows, 0)

    def make_block(owner, slot):
        col_aug[0:feat, :] = points[owner]
        col_aug[feat:, :] = norm_rows(points[owner], False)

        def step(i, carry):
            at = pl.multiple_of(i * CHUNK, CHUNK)
            kernel_store[slot, pl.ds(at, CHUNK), :] = entries(col_aug, at, own_aug).astype(jnp.bfloat16)
            return carry

        lax.fori_loop(0, local // CHUNK, step, 0)

    own_points = pltpu.make_async_copy(points_ref, own_slot, chol_sem)
    chol_copy.wait()
    own_points.start()
    own_points.wait()

    row = lax.broadcasted_iota(jnp.int32, (TILE, TILE), 0)
    col = lax.broadcasted_iota(jnp.int32, (TILE, TILE), 1)

    blocks = [chol[b * TILE:(b + 1) * TILE, b * TILE:(b + 1) * TILE] for b in range(tiles)]
    for b in range(tiles):
        inverse[b] = jnp.where(row == col, 1.0 / blocks[b], 0.0)
    size = 1
    while size < TILE:
        below = (row // size == col // size + 1) & (row // (2 * size) == col // (2 * size))
        for b in range(tiles):
            off = jnp.where(below, chol[b * TILE:(b + 1) * TILE, b * TILE:(b + 1) * TILE], 0.0)
            if size == 1:
                on_row = jnp.sum(inverse[b], axis=1, keepdims=True)
                on_col = jnp.sum(inverse[b], axis=0, keepdims=True)
                change = on_row * off * on_col
            else:
                change = dot_nn(dot_nn(inverse[b], off, HIGH), inverse[b], HIGH)
            inverse[b] = inverse[b] - change
        size *= 2
    for b in range(groups):
        upper, lower = inverse[2 * b], inverse[2 * b + 1]
        at, end = b * GROUP, (b + 1) * GROUP
        off = chol[at + TILE:end, at:at + TILE]
        change = dot_nn(dot_nn(lower, off, HIGH), upper, HIGH)
        zero = jnp.zeros_like(upper)
        whole = jnp.concatenate(
            [jnp.concatenate([upper, zero], axis=1), jnp.concatenate([-change, lower], axis=1)], axis=0
        )
        store_split(inverse_parts, (b,), whole)
        if b > 0:
            store_split(chol_parts, (slice(at, end), slice(0, at)), chol[at:end, :at])

    wait_all(lambda to: rs_send.at[to], rs_recv, rs_sems)
    ag[me] = jnp.sum(rs_recv[...], axis=0)
    send_all(lambda to: ag.at[me], ag, ag_sems)

    if keep:
        make_block(me, me)

    def relay(s, both):
        near = row_of(pos - s, 0)
        remote(points_ref, points.at[near], point_fwd.at[near], point_recv.at[near], right).wait_recv()
        if both:
            remote(points.at[near], points.at[near], point_fwd.at[near], point_recv.at[near], right).start()
        remote(points.at[near], points.at[near], point_side.at[near], point_recv.at[near], partner).start()
        if both:
            far = row_of(pos + s, 0)
            remote(points_ref, points.at[far], point_fwd.at[far], point_recv.at[far], left).wait_recv()
            remote(points.at[far], points.at[far], point_side.at[far], point_recv.at[far], partner).start()

            @pl.when(s < half - 1)
            def _():
                remote(points.at[far], points.at[far], point_fwd.at[far], point_recv.at[far], left).start()

        def build(lane):
            def one(way, carry):
                owner = row_of(pos - s + 2 * s * way, lane)
                if lane == 1:
                    remote(points_ref, points.at[owner], point_side.at[owner], point_recv.at[owner], partner).wait_recv()
                if keep:
                    make_block(owner, owner)
                return carry

            lax.fori_loop(0, 2 if both else 1, one, 0)

        build(0)
        build(1)

    relay(1, True)
    remote(points_ref, points.at[partner], point_side.at[partner], point_recv.at[partner], partner).wait_recv()

    wait_all(lambda to: ag.at[me], ag, ag_sems)
    for piece in range(n):
        h, j = piece // tiles, piece % tiles
        work[h * rows_per:(h + 1) * rows_per, j * TILE:(j + 1) * TILE] = ag[piece]
    pieces = [work[:, b * GROUP:(b + 1) * GROUP] for b in range(groups)]

    def block_parts(i, j):
        rows, cols = slice(i * GROUP, (i + 1) * GROUP), slice(j * GROUP, (j + 1) * GROUP)
        return [chol_parts[term, rows, cols] for term in range(3)]

    def inverse_of(b):
        return [inverse_parts[term, b] for term in range(3)]

    for b in range(groups):
        pieces[b] = dot_split(pieces[b], inverse_of(b), dot_nt)
        for i in range(b + 1, groups):
            pieces[i] = pieces[i] - dot_split(pieces[b], block_parts(i, b), dot_nt)
    for b in reversed(range(groups)):
        pieces[b] = dot_split(pieces[b], inverse_of(b), dot_nn)
        for j in reversed(range(b)):
            pieces[j] = pieces[j] - dot_split(pieces[b], block_parts(b, j), dot_nn)
    coeffs = jnp.concatenate(pieces, axis=1)

    ridge = ridge_ref[0]
    residual = residual_ref[...]
    precond = (residual - dot_split(coeffs, [cross_t.at[term][...] for term in range(3)], dot_nn)) / ridge
    inner_buf[me] = to_row(jnp.sum(precond * residual, axis=1, keepdims=True), TILE)
    send_all(lambda to: inner_buf.at[me], inner_buf, inner_sems)

    if keep:
        make_block(partner, partner)
    lax.fori_loop(2, min(3, half), lambda s, carry: (relay(s, True), carry)[1], 0)
    wait_all(lambda to: inner_buf.at[me], inner_buf, inner_sems)
    inner_row = jnp.sum(inner_buf[...], axis=0)
    inner_out[...] = inner_row[:, :outs]
    inner = to_column(inner_row)
    direction_new = precond + (inner / to_column(rz_ref[...])) * direction_ref[...]
    direction_out[...] = direction_new
    dirs[me] = direction_new.astype(jnp.bfloat16)
    send_all(lambda to: dirs.at[me], dirs, dir_sems)

    lax.fori_loop(3, half, lambda s, carry: (relay(s, True), carry)[1], 0)
    relay(half, False)

    def image_part(owner, slot):
        if not keep:
            make_block(owner, slot)
        proj[...] += dot_nn(dirs[owner], kernel_store[slot])

    proj[...] = jnp.zeros_like(proj)
    image_part(me, me if keep else 0)

    def gather_image(to):
        remote(dirs.at[me], dirs.at[to], dir_sems.at[0, to], dir_sems.at[1, to], to).wait_recv()
        image_part(to, to if keep else 0)

    others(gather_image)

    direction_new = direction_out[...]
    image = proj[...] + ridge * direction_new
    image_out[...] = image
    curv_buf[me] = to_row(jnp.sum(direction_new * image, axis=1, keepdims=True), TILE)
    send_all(lambda to: curv_buf.at[me], curv_buf, curv_sems)

    drain(lambda to: rs_send.at[to], rs_recv, rs_sems)
    drain(lambda to: ag.at[me], ag, ag_sems)
    drain(lambda to: inner_buf.at[me], inner_buf, inner_sems)
    drain(lambda to: dirs.at[me], dirs, dir_sems)
    first_right.wait_send()
    first_left.wait_send()
    first_side.wait_send()

    def relay_drain(s, both):
        near = row_of(pos - s, 0)
        remote(points.at[near], points.at[near], point_side.at[near], point_recv.at[near], partner).wait_send()
        if both:
            remote(points.at[near], points.at[near], point_fwd.at[near], point_recv.at[near], right).wait_send()
            far = row_of(pos + s, 0)
            remote(points.at[far], points.at[far], point_side.at[far], point_recv.at[far], partner).wait_send()

            @pl.when(s < half - 1)
            def _():
                remote(points.at[far], points.at[far], point_fwd.at[far], point_recv.at[far], left).wait_send()

    lax.fori_loop(1, half, lambda s, carry: (relay_drain(s, True), carry)[1], 0)
    relay_drain(half, False)

    wait_all(lambda to: curv_buf.at[me], curv_buf, curv_sems)
    alpha_out[...] = inner_out[...] / jnp.sum(curv_buf[...], axis=0)[:, :outs]
    drain(lambda to: curv_buf.at[me], curv_buf, curv_sems)


def finish(
    image_ref,
    direction_ref,
    inner_ref,
    alpha_ref,
    solution_ref,
    residual_ref,
    solution_out,
    residual_out,
    direction_out,
    inner_out,
):
    alpha = to_column(alpha_ref[...])
    direction = direction_ref[...]
    solution_out[...] = solution_ref[...] + alpha * direction
    residual_out[...] = residual_ref[...] - alpha * image_ref[...]
    direction_out[...] = direction
    inner_out[...] = inner_ref[...]


def solution(mesh):
    n = mesh.shape["rows"]

    def local(points, landmarks, chol, ridge, solution, residual, direction, rz_prev):
        feat, own = points.shape
        land = landmarks.shape[1]
        outs = residual.shape[0]
        keep = n <= STORED_BLOCKS
        piece = outs * land // (TILE * n)
        f32, bf16 = jnp.float32, jnp.bfloat16
        vmem = pl.BlockSpec(memory_space=pltpu.VMEM)
        wide = jax.ShapeDtypeStruct((outs, own), f32)
        thin = jax.ShapeDtypeStruct((1, outs), f32)
        dma = pltpu.SemaphoreType.DMA
        results = pl.pallas_call(
            functools.partial(kernel, n, keep),
            out_shape=(wide, wide, thin, thin),
            in_specs=[
                vmem,
                vmem,
                pl.BlockSpec(memory_space=pl.ANY),
                pl.BlockSpec(memory_space=pltpu.SMEM),
                vmem,
                vmem,
                vmem,
            ],
            out_specs=(vmem,) * 4,
            scratch_shapes=[
                pltpu.VMEM((land, land), f32),
                pltpu.VMEM((3, land, land), bf16),
                pltpu.VMEM((3, land // GROUP, GROUP, GROUP), bf16),
                pltpu.VMEM((land // TILE, TILE, TILE), f32),
                pltpu.VMEM((n, feat, own), bf16),
                pltpu.VMEM((feat + 16, own), bf16),
                pltpu.VMEM((feat + 16, own), bf16),
                pltpu.VMEM((3, land, own), bf16),
                pltpu.VMEM((n if keep else 1, own, own), bf16),
                pltpu.VMEM((n, piece, TILE), f32),
                pltpu.VMEM((n, piece, TILE), f32),
                pltpu.VMEM((n, piece, TILE), f32),
                pltpu.VMEM((outs, land), f32),
                pltpu.VMEM((outs, land), f32),
                pltpu.VMEM((n, 1, TILE), f32),
                pltpu.VMEM((n, outs, own), bf16),
                pltpu.VMEM((n, 1, TILE), f32),
                dma,
                dma((2, n)),
                dma((2, n)),
                dma((2, n)),
                dma((2, n)),
                dma((2, n)),
                dma((n,)),
                dma((n,)),
                dma((n,)),
                dma,
            ],
            compiler_params=pltpu.CompilerParams(
                collective_id=0, has_side_effects=True, vmem_limit_bytes=62 * 1024 * 1024
            ),
            name="cg_step",
        )(points, landmarks, chol, ridge, residual, direction, rz_prev.reshape(1, outs))
        results = pl.pallas_call(
            finish,
            out_shape=(wide, wide, wide, thin),
            in_specs=[vmem] * 6,
            out_specs=(vmem,) * 4,
            name="finish",
        )(*results, solution, residual)
        return (results[0], results[1], results[2], results[3].reshape(outs))

    wide_spec = P(None, ("groups", "rows"))
    in_specs = (
        wide_spec,
        P(None, "groups"),
        P("groups", None),
        P("groups"),
        wide_spec,
        wide_spec,
        wide_spec,
        P("groups"),
    )
    out_specs = (wide_spec, wide_spec, wide_spec, P("groups"))
    return jax.shard_map(local, mesh=mesh, in_specs=in_specs, out_specs=out_specs, check_vma=False)
```

```python
import functools
import math

import jax
import jax.numpy as jnp
from jax import lax
from jax.experimental import pallas as pl
from jax.experimental.pallas import tpu as pltpu
from jax.sharding import PartitionSpec as P

HIGH = lax.Precision.HIGHEST
TILE = 128
CHUNK = 256
GROUP = 2 * TILE
STORED_BLOCKS = 16


def dot_nn(left, right, precision=None):
    return lax.dot_general(
        left, right, (((1,), (0,)), ((), ())), precision=precision, preferred_element_type=jnp.float32
    )


def dot_nt(left, right, precision=None):
    return lax.dot_general(
        left, right, (((1,), (1,)), ((), ())), precision=precision, preferred_element_type=jnp.float32
    )


def dot_tn(left, right):
    return lax.dot_general(
        left, right, (((0,), (0,)), ((), ())), preferred_element_type=jnp.float32
    )


def split(values):
    top = values.astype(jnp.bfloat16).astype(jnp.float32)
    rest = values - top
    mid = rest.astype(jnp.bfloat16).astype(jnp.float32)
    return top, mid, rest - mid


def store_split(ref, at, values):
    for term, part in enumerate(split(values)):
        ref[(term,) + at] = part.astype(jnp.bfloat16)


def dot_split(left, parts, dot):
    outs = left.shape[0]
    stacked = jnp.concatenate(split(left), axis=0).astype(jnp.bfloat16)
    high = dot(stacked, parts[0])
    mid = dot(stacked[:2 * outs], parts[1])
    low = dot(stacked[:2 * outs], parts[2])
    small = low[:outs] + mid[outs:] + high[2 * outs:]
    return high[:outs] + (high[outs:2 * outs] + mid[:outs] + small)


def norm_rows(features, first):
    wide = features.astype(jnp.float32)
    half = -0.5 * jnp.sum(wide * wide, axis=0, keepdims=True)
    top = half.astype(jnp.bfloat16).astype(jnp.float32)
    rest = half - top
    mid = rest.astype(jnp.bfloat16).astype(jnp.float32)
    low = rest - mid
    row = lax.broadcasted_iota(jnp.int32, (16, features.shape[1]), 0)
    at = 0 if first else 3
    ones = 3 - at
    rows = jnp.where((row >= ones) & (row < ones + 3), 1.0, 0.0)
    rows = jnp.where(row == at, top, rows)
    rows = jnp.where(row == at + 1, mid, rows)
    rows = jnp.where(row == at + 2, low, rows)
    return rows.astype(jnp.bfloat16)


def eye_mask(width):
    shape = (8, width)
    return lax.broadcasted_iota(jnp.int32, shape, 0) == lax.broadcasted_iota(jnp.int32, shape, 1)


def to_row(column, width):
    return jnp.sum(jnp.where(eye_mask(width), column, 0.0), axis=0, keepdims=True)


def to_column(row):
    return jnp.sum(jnp.where(eye_mask(row.shape[1]), row, 0.0), axis=1, keepdims=True)


def kernel(
    n,
    keep,
    points_ref,
    landmarks_ref,
    chol_hbm,
    ridge_ref,
    residual_ref,
    direction_ref,
    rz_ref,
    image_out,
    direction_out,
    inner_out,
    alpha_out,
    chol,
    chol_parts,
    inverse_parts,
    inverse,
    points,
    own_aug,
    col_aug,
    cross_t,
    kernel_store,
    rs_send,
    rs_recv,
    ag,
    proj,
    work,
    inner_buf,
    dirs,
    curv_buf,
    chol_sem,
    rs_sems,
    ag_sems,
    inner_sems,
    dir_sems,
    curv_sems,
    point_recv,
    point_fwd,
    point_side,
    point_back,
    share_sems,
):
    me = lax.axis_index("rows")
    feat, local = points_ref.shape
    land = landmarks_ref.shape[1]
    outs = residual_ref.shape[0]
    chips = n // 2
    half = chips // 2
    core = me % 2
    chip = me // 2
    odd = chip % 2
    pos = (1 - odd) * (chip // 2) + odd * (chips - (chip + 1) // 2)
    scale = math.log2(math.e) / feat

    def row_of(position, lane):
        position = (position + chips) % chips
        upper = position // half
        at = (1 - upper) * (2 * position) + upper * (2 * chips - 1 - 2 * position)
        return at * 2 + (core + lane) % 2

    def remote(src, dst, send, recv, to):
        return pltpu.make_async_remote_copy(
            src_ref=src,
            dst_ref=dst,
            send_sem=send,
            recv_sem=recv,
            device_id={"rows": to},
            device_id_type=pl.DeviceIdType.MESH,
        )

    def others(body):
        lax.fori_loop(1, n, lambda k, carry: (body((me + k) % n), carry)[1], 0)

    def send_all(src_of, buf, sems):
        others(lambda to: remote(src_of(to), buf.at[me], sems.at[0, to], sems.at[1, me], to).start())

    def wait_all(src_of, buf, sems):
        others(lambda to: remote(src_of(to), buf.at[to], sems.at[0, to], sems.at[1, to], to).wait_recv())

    def drain(src_of, buf, sems):
        others(lambda to: remote(src_of(to), buf.at[me], sems.at[0, to], sems.at[1, me], to).wait_send())

    chol_copy = pltpu.make_async_copy(chol_hbm, chol, chol_sem)
    chol_copy.start()

    barrier = pltpu.get_barrier_semaphore()
    others(lambda to: pl.semaphore_signal(
        barrier, inc=1, device_id={"rows": to}, device_id_type=pl.DeviceIdType.MESH))

    right = row_of(pos + 1, 0)
    left = row_of(pos - 1, 0)
    partner = row_of(pos, 1)
    own_slot = points.at[me]
    first_right = remote(points_ref, own_slot, point_fwd.at[me], point_recv.at[me], right)
    first_left = remote(points_ref, own_slot, point_back, point_recv.at[me], left)
    first_side = remote(points_ref, own_slot, point_side.at[me], point_recv.at[me], partner)

    own_aug[0:feat, :] = points_ref[...]
    own_aug[feat:, :] = norm_rows(points_ref[...], True)
    col_aug[0:feat, :] = landmarks_ref[...]
    col_aug[feat:, :] = norm_rows(landmarks_ref[...], False)

    def entries(left_aug, at, right_aug):
        return jnp.exp2(dot_tn(left_aug[:, pl.ds(at, CHUNK)], right_aug[...]) * scale)

    proj[...] = jnp.zeros_like(proj)

    def project(i, carry):
        at = pl.multiple_of(i * CHUNK, CHUNK)
        parts = [part.astype(jnp.bfloat16) for part in split(entries(own_aug, at, col_aug))]
        proj[...] += dot_split(residual_ref[:, pl.ds(at, CHUNK)], parts, dot_nn)
        return carry

    lax.fori_loop(0, local // CHUNK, project, 0)

    pl.semaphore_wait(barrier, n - 1)

    tiles = land // TILE
    groups = land // GROUP
    rows_per = outs * tiles // n
    for piece in range(n):
        h, j = piece // tiles, piece % tiles
        rs_send[piece] = proj[h * rows_per:(h + 1) * rows_per, j * TILE:(j + 1) * TILE]
    send_all(lambda to: rs_send.at[to], rs_recv, rs_sems)
    rs_recv[me] = rs_send[me]
    first_right.start()
    first_left.start()
    first_side.start()

    def landmark_rows(i, carry):
        at = pl.multiple_of(i * CHUNK, CHUNK)
        store_split(cross_t, (pl.ds(at, CHUNK), slice(None)), entries(col_aug, at, own_aug))
        return carry

    lax.fori_loop(0, land // CHUNK, landmark_rows, 0)

    def make_block(owner, slot):
        col_aug[0:feat, :] = points[owner]
        col_aug[feat:, :] = norm_rows(points[owner], False)

        for at in range(0, local, CHUNK):
            kernel_store[slot, at:at + CHUNK, :] = entries(col_aug, at, own_aug).astype(jnp.bfloat16)

    own_points = pltpu.make_async_copy(points_ref, own_slot, chol_sem)
    chol_copy.wait()
    own_points.start()
    own_points.wait()

    row = lax.broadcasted_iota(jnp.int32, (TILE, TILE), 0)
    col = lax.broadcasted_iota(jnp.int32, (TILE, TILE), 1)

    share = tiles // 2
    first = core * share

    def own_block(b):
        at = pl.multiple_of((first + b) * TILE, TILE)
        return chol[pl.ds(at, TILE), pl.ds(at, TILE)]

    inverted = [jnp.where(row == col, 1.0 / own_block(b), 0.0) for b in range(share)]
    size = 1
    while size < TILE:
        below = (row // size == col // size + 1) & (row // (2 * size) == col // (2 * size))
        for b in range(share):
            off = jnp.where(below, own_block(b), 0.0)
            if size == 1:
                on_row = jnp.sum(inverted[b], axis=1, keepdims=True)
                on_col = jnp.sum(inverted[b], axis=0, keepdims=True)
                change = on_row * off * on_col
            else:
                change = dot_nn(dot_nn(inverted[b], off, HIGH), inverted[b], HIGH)
            inverted[b] = inverted[b] - change
        size *= 2
    for b in range(share):
        inverse[first + b] = inverted[b]

    wait_all(lambda to: rs_send.at[to], rs_recv, rs_sems)
    ag[me] = jnp.sum(rs_recv[...], axis=0)
    send_all(lambda to: ag.at[me], ag, ag_sems)

    shares = inverse.at[pl.ds(first, share)]
    shared = remote(shares, shares, share_sems.at[0], share_sems.at[1], partner)
    shared.start()

    if keep:
        make_block(me, me)

    def relay(s, both):
        near = row_of(pos - s, 0)
        remote(points_ref, points.at[near], point_fwd.at[near], point_recv.at[near], right).wait_recv()
        if both:
            remote(points.at[near], points.at[near], point_fwd.at[near], point_recv.at[near], right).start()
        remote(points.at[near], points.at[near], point_side.at[near], point_recv.at[near], partner).start()
        if both:
            far = row_of(pos + s, 0)
            remote(points_ref, points.at[far], point_fwd.at[far], point_recv.at[far], left).wait_recv()
            remote(points.at[far], points.at[far], point_side.at[far], point_recv.at[far], partner).start()

            @pl.when(s < half - 1)
            def _():
                remote(points.at[far], points.at[far], point_fwd.at[far], point_recv.at[far], left).start()

        def build(lane):
            def one(way, carry):
                owner = row_of(pos - s + 2 * s * way, lane)
                if lane == 1:
                    remote(points_ref, points.at[owner], point_side.at[owner], point_recv.at[owner], partner).wait_recv()
                if keep:
                    make_block(owner, owner)
                return carry

            lax.fori_loop(0, 2 if both else 1, one, 0)

        build(0)
        build(1)

    relay(1, True)
    remote(points_ref, points.at[partner], point_side.at[partner], point_recv.at[partner], partner).wait_recv()

    other = inverse.at[pl.ds(share - first, share)]
    remote(other, other, share_sems.at[0], share_sems.at[1], partner).wait_recv()
    for b in range(groups):
        upper, lower = inverse[2 * b], inverse[2 * b + 1]
        at, end = b * GROUP, (b + 1) * GROUP
        off = chol[at + TILE:end, at:at + TILE]
        change = dot_nn(dot_nn(lower, off, HIGH), upper, HIGH)
        zero = jnp.zeros_like(upper)
        whole = jnp.concatenate(
            [jnp.concatenate([upper, zero], axis=1), jnp.concatenate([-change, lower], axis=1)], axis=0
        )
        store_split(inverse_parts, (b,), whole)
        if b > 0:
            store_split(chol_parts, (slice(at, end), slice(0, at)), chol[at:end, :at])

    wait_all(lambda to: ag.at[me], ag, ag_sems)
    for piece in range(n):
        h, j = piece // tiles, piece % tiles
        work[h * rows_per:(h + 1) * rows_per, j * TILE:(j + 1) * TILE] = ag[piece]
    pieces = [work[:, b * GROUP:(b + 1) * GROUP] for b in range(groups)]

    def block_parts(i, j):
        rows, cols = slice(i * GROUP, (i + 1) * GROUP), slice(j * GROUP, (j + 1) * GROUP)
        return [chol_parts[term, rows, cols] for term in range(3)]

    def inverse_of(b):
        return [inverse_parts[term, b] for term in range(3)]

    for b in range(groups):
        pieces[b] = dot_split(pieces[b], inverse_of(b), dot_nt)
        for i in range(b + 1, groups):
            pieces[i] = pieces[i] - dot_split(pieces[b], block_parts(i, b), dot_nt)
    for b in reversed(range(groups)):
        pieces[b] = dot_split(pieces[b], inverse_of(b), dot_nn)
        for j in reversed(range(b)):
            pieces[j] = pieces[j] - dot_split(pieces[b], block_parts(b, j), dot_nn)
    coeffs = jnp.concatenate(pieces, axis=1)

    ridge = ridge_ref[0]
    residual = residual_ref[...]
    precond = (residual - dot_split(coeffs, [cross_t.at[term][...] for term in range(3)], dot_nn)) / ridge
    inner_buf[me] = to_row(jnp.sum(precond * residual, axis=1, keepdims=True), TILE)
    send_all(lambda to: inner_buf.at[me], inner_buf, inner_sems)

    if keep:
        make_block(partner, partner)
    lax.fori_loop(2, min(3, half), lambda s, carry: (relay(s, True), carry)[1], 0)
    wait_all(lambda to: inner_buf.at[me], inner_buf, inner_sems)
    inner_row = jnp.sum(inner_buf[...], axis=0)
    inner_out[...] = inner_row[:, :outs]
    inner = to_column(inner_row)
    direction_new = precond + (inner / to_column(rz_ref[...])) * direction_ref[...]
    direction_out[...] = direction_new
    dirs[me] = direction_new.astype(jnp.bfloat16)
    send_all(lambda to: dirs.at[me], dirs, dir_sems)

    lax.fori_loop(3, half, lambda s, carry: (relay(s, True), carry)[1], 0)
    relay(half, False)

    def image_part(owner, slot):
        if not keep:
            make_block(owner, slot)
        proj[...] += dot_nn(dirs[owner], kernel_store[slot])

    proj[...] = jnp.zeros_like(proj)
    image_part(me, me if keep else 0)

    def gather_image(to):
        remote(dirs.at[me], dirs.at[to], dir_sems.at[0, to], dir_sems.at[1, to], to).wait_recv()
        image_part(to, to if keep else 0)

    others(gather_image)

    direction_new = direction_out[...]
    image = proj[...] + ridge * direction_new
    image_out[...] = image
    curv_buf[me] = to_row(jnp.sum(direction_new * image, axis=1, keepdims=True), TILE)
    send_all(lambda to: curv_buf.at[me], curv_buf, curv_sems)

    drain(lambda to: rs_send.at[to], rs_recv, rs_sems)
    drain(lambda to: ag.at[me], ag, ag_sems)
    drain(lambda to: inner_buf.at[me], inner_buf, inner_sems)
    drain(lambda to: dirs.at[me], dirs, dir_sems)
    shared.wait_send()
    first_right.wait_send()
    first_left.wait_send()
    first_side.wait_send()

    def relay_drain(s, both):
        near = row_of(pos - s, 0)
        remote(points.at[near], points.at[near], point_side.at[near], point_recv.at[near], partner).wait_send()
        if both:
            remote(points.at[near], points.at[near], point_fwd.at[near], point_recv.at[near], right).wait_send()
            far = row_of(pos + s, 0)
            remote(points.at[far], points.at[far], point_side.at[far], point_recv.at[far], partner).wait_send()

            @pl.when(s < half - 1)
            def _():
                remote(points.at[far], points.at[far], point_fwd.at[far], point_recv.at[far], left).wait_send()

    lax.fori_loop(1, half, lambda s, carry: (relay_drain(s, True), carry)[1], 0)
    relay_drain(half, False)

    wait_all(lambda to: curv_buf.at[me], curv_buf, curv_sems)
    alpha_out[...] = inner_out[...] / jnp.sum(curv_buf[...], axis=0)[:, :outs]
    drain(lambda to: curv_buf.at[me], curv_buf, curv_sems)


def finish(
    image_ref,
    direction_ref,
    inner_ref,
    alpha_ref,
    solution_ref,
    residual_ref,
    solution_out,
    residual_out,
    direction_out,
    inner_out,
):
    alpha = to_column(alpha_ref[...])
    direction = direction_ref[...]
    solution_out[...] = solution_ref[...] + alpha * direction
    residual_out[...] = residual_ref[...] - alpha * image_ref[...]
    direction_out[...] = direction
    inner_out[...] = inner_ref[...]


def solution(mesh):
    n = mesh.shape["rows"]

    def local(points, landmarks, chol, ridge, solution, residual, direction, rz_prev):
        feat, own = points.shape
        land = landmarks.shape[1]
        outs = residual.shape[0]
        keep = n <= STORED_BLOCKS
        piece = outs * land // (TILE * n)
        f32, bf16 = jnp.float32, jnp.bfloat16
        vmem = pl.BlockSpec(memory_space=pltpu.VMEM)
        wide = jax.ShapeDtypeStruct((outs, own), f32)
        thin = jax.ShapeDtypeStruct((1, outs), f32)
        dma = pltpu.SemaphoreType.DMA
        results = pl.pallas_call(
            functools.partial(kernel, n, keep),
            out_shape=(wide, wide, thin, thin),
            in_specs=[
                vmem,
                vmem,
                pl.BlockSpec(memory_space=pl.ANY),
                pl.BlockSpec(memory_space=pltpu.SMEM),
                vmem,
                vmem,
                vmem,
            ],
            out_specs=(vmem,) * 4,
            scratch_shapes=[
                pltpu.VMEM((land, land), f32),
                pltpu.VMEM((3, land, land), bf16),
                pltpu.VMEM((3, land // GROUP, GROUP, GROUP), bf16),
                pltpu.VMEM((land // TILE, TILE, TILE), f32),
                pltpu.VMEM((n, feat, own), bf16),
                pltpu.VMEM((feat + 16, own), bf16),
                pltpu.VMEM((feat + 16, own), bf16),
                pltpu.VMEM((3, land, own), bf16),
                pltpu.VMEM((n if keep else 1, own, own), bf16),
                pltpu.VMEM((n, piece, TILE), f32),
                pltpu.VMEM((n, piece, TILE), f32),
                pltpu.VMEM((n, piece, TILE), f32),
                pltpu.VMEM((outs, land), f32),
                pltpu.VMEM((outs, land), f32),
                pltpu.VMEM((n, 1, TILE), f32),
                pltpu.VMEM((n, outs, own), bf16),
                pltpu.VMEM((n, 1, TILE), f32),
                dma,
                dma((2, n)),
                dma((2, n)),
                dma((2, n)),
                dma((2, n)),
                dma((2, n)),
                dma((n,)),
                dma((n,)),
                dma((n,)),
                dma,
                dma((2,)),
            ],
            compiler_params=pltpu.CompilerParams(
                collective_id=0, has_side_effects=True, vmem_limit_bytes=62 * 1024 * 1024
            ),
            name="cg_step",
        )(points, landmarks, chol, ridge, residual, direction, rz_prev.reshape(1, outs))
        results = pl.pallas_call(
            finish,
            out_shape=(wide, wide, wide, thin),
            in_specs=[vmem] * 6,
            out_specs=(vmem,) * 4,
            name="finish",
        )(*results, solution, residual)
        return (results[0], results[1], results[2], results[3].reshape(outs))

    wide_spec = P(None, ("groups", "rows"))
    in_specs = (
        wide_spec,
        P(None, "groups"),
        P("groups", None),
        P("groups"),
        wide_spec,
        wide_spec,
        wide_spec,
        P("groups"),
    )
    out_specs = (wide_spec, wide_spec, wide_spec, P("groups"))
    return jax.shard_map(local, mesh=mesh, in_specs=in_specs, out_specs=out_specs, check_vma=False)
```

```python
import functools
import math

import jax
import jax.numpy as jnp
from jax import lax
from jax.experimental import pallas as pl
from jax.experimental.pallas import tpu as pltpu
from jax.sharding import PartitionSpec as P

HIGH = lax.Precision.HIGHEST
TILE = 128
CHUNK = 256
GROUP = 2 * TILE
STORED_BLOCKS = 16


def dot_nn(left, right, precision=None):
    return lax.dot_general(
        left, right, (((1,), (0,)), ((), ())), precision=precision, preferred_element_type=jnp.float32
    )


def dot_nt(left, right, precision=None):
    return lax.dot_general(
        left, right, (((1,), (1,)), ((), ())), precision=precision, preferred_element_type=jnp.float32
    )


def dot_tn(left, right):
    return lax.dot_general(
        left, right, (((0,), (0,)), ((), ())), preferred_element_type=jnp.float32
    )


def split(values):
    top = values.astype(jnp.bfloat16).astype(jnp.float32)
    rest = values - top
    mid = rest.astype(jnp.bfloat16).astype(jnp.float32)
    return top, mid, rest - mid


def store_split(ref, at, values):
    for term, part in enumerate(split(values)):
        ref[(term,) + at] = part.astype(jnp.bfloat16)


def dot_split(left, parts, dot):
    outs = left.shape[0]
    stacked = jnp.concatenate(split(left), axis=0).astype(jnp.bfloat16)
    high = dot(stacked, parts[0])
    mid = dot(stacked[:2 * outs], parts[1])
    low = dot(stacked[:2 * outs], parts[2])
    small = low[:outs] + mid[outs:] + high[2 * outs:]
    return high[:outs] + (high[outs:2 * outs] + mid[:outs] + small)


def norm_rows(features, first):
    wide = features.astype(jnp.float32)
    half = -0.5 * jnp.sum(wide * wide, axis=0, keepdims=True)
    top = half.astype(jnp.bfloat16).astype(jnp.float32)
    rest = half - top
    mid = rest.astype(jnp.bfloat16).astype(jnp.float32)
    low = rest - mid
    row = lax.broadcasted_iota(jnp.int32, (16, features.shape[1]), 0)
    at = 0 if first else 3
    ones = 3 - at
    rows = jnp.where((row >= ones) & (row < ones + 3), 1.0, 0.0)
    rows = jnp.where(row == at, top, rows)
    rows = jnp.where(row == at + 1, mid, rows)
    rows = jnp.where(row == at + 2, low, rows)
    return rows.astype(jnp.bfloat16)


def eye_mask(width):
    shape = (8, width)
    return lax.broadcasted_iota(jnp.int32, shape, 0) == lax.broadcasted_iota(jnp.int32, shape, 1)


def to_row(column, width):
    return jnp.sum(jnp.where(eye_mask(width), column, 0.0), axis=0, keepdims=True)


def to_column(row):
    return jnp.sum(jnp.where(eye_mask(row.shape[1]), row, 0.0), axis=1, keepdims=True)


def kernel(
    n,
    keep,
    points_ref,
    landmarks_ref,
    chol_hbm,
    ridge_ref,
    residual_ref,
    direction_ref,
    rz_ref,
    image_out,
    direction_out,
    inner_out,
    alpha_out,
    chol,
    chol_parts,
    inverse_parts,
    inverse,
    points,
    own_aug,
    col_aug,
    cross_t,
    kernel_store,
    rs_send,
    rs_recv,
    ag,
    proj,
    work,
    inner_buf,
    dirs,
    curv_buf,
    chol_sem,
    rs_sems,
    ag_sems,
    inner_sems,
    dir_sems,
    curv_sems,
    point_recv,
    point_fwd,
    point_side,
    point_back,
    share_sems,
):
    me = lax.axis_index("rows")
    feat, local = points_ref.shape
    land = landmarks_ref.shape[1]
    outs = residual_ref.shape[0]
    chips = n // 2
    half = chips // 2
    core = me % 2
    chip = me // 2
    odd = chip % 2
    pos = (1 - odd) * (chip // 2) + odd * (chips - (chip + 1) // 2)
    scale = math.log2(math.e) / feat

    def row_of(position, lane):
        position = (position + chips) % chips
        upper = position // half
        at = (1 - upper) * (2 * position) + upper * (2 * chips - 1 - 2 * position)
        return at * 2 + (core + lane) % 2

    def remote(src, dst, send, recv, to):
        return pltpu.make_async_remote_copy(
            src_ref=src,
            dst_ref=dst,
            send_sem=send,
            recv_sem=recv,
            device_id={"rows": to},
            device_id_type=pl.DeviceIdType.MESH,
        )

    def others(body):
        lax.fori_loop(1, n, lambda k, carry: (body((me + k) % n), carry)[1], 0)

    def send_all(src_of, buf, sems):
        others(lambda to: remote(src_of(to), buf.at[me], sems.at[0, to], sems.at[1, me], to).start())

    def wait_all(src_of, buf, sems):
        others(lambda to: remote(src_of(to), buf.at[to], sems.at[0, to], sems.at[1, to], to).wait_recv())

    def drain(src_of, buf, sems):
        others(lambda to: remote(src_of(to), buf.at[me], sems.at[0, to], sems.at[1, me], to).wait_send())

    chol_copy = pltpu.make_async_copy(chol_hbm, chol, chol_sem)
    chol_copy.start()

    barrier = pltpu.get_barrier_semaphore()
    others(lambda to: pl.semaphore_signal(
        barrier, inc=1, device_id={"rows": to}, device_id_type=pl.DeviceIdType.MESH))

    right = row_of(pos + 1, 0)
    left = row_of(pos - 1, 0)
    partner = row_of(pos, 1)
    own_slot = points.at[me]
    first_right = remote(points_ref, own_slot, point_fwd.at[me], point_recv.at[me], right)
    first_left = remote(points_ref, own_slot, point_back, point_recv.at[me], left)
    first_side = remote(points_ref, own_slot, point_side.at[me], point_recv.at[me], partner)

    own_aug[0:feat, :] = points_ref[...]
    own_aug[feat:, :] = norm_rows(points_ref[...], True)
    col_aug[0:feat, :] = landmarks_ref[...]
    col_aug[feat:, :] = norm_rows(landmarks_ref[...], False)

    def entries(left_aug, at, right_aug):
        return jnp.exp2(dot_tn(left_aug[:, pl.ds(at, CHUNK)], right_aug[...]) * scale)

    proj[...] = jnp.zeros_like(proj)

    def project(i, carry):
        at = pl.multiple_of(i * CHUNK, CHUNK)
        parts = [part.astype(jnp.bfloat16) for part in split(entries(own_aug, at, col_aug))]
        proj[...] += dot_split(residual_ref[:, pl.ds(at, CHUNK)], parts, dot_nn)
        return carry

    lax.fori_loop(0, local // CHUNK, project, 0)

    pl.semaphore_wait(barrier, n - 1)

    tiles = land // TILE
    groups = land // GROUP
    rows_per = outs * tiles // n
    for piece in range(n):
        h, j = piece // tiles, piece % tiles
        rs_send[piece] = proj[h * rows_per:(h + 1) * rows_per, j * TILE:(j + 1) * TILE]
    send_all(lambda to: rs_send.at[to], rs_recv, rs_sems)
    rs_recv[me] = rs_send[me]
    first_right.start()
    first_left.start()
    first_side.start()

    def landmark_rows(i, carry):
        at = pl.multiple_of(i * CHUNK, CHUNK)
        store_split(cross_t, (pl.ds(at, CHUNK), slice(None)), entries(col_aug, at, own_aug))
        return carry

    lax.fori_loop(0, land // CHUNK, landmark_rows, 0)

    def make_block(owner, slot):
        col_aug[0:feat, :] = points[owner]
        col_aug[feat:, :] = norm_rows(points[owner], False)

        for at in range(0, local, CHUNK):
            kernel_store[slot, at:at + CHUNK, :] = entries(col_aug, at, own_aug).astype(jnp.bfloat16)

    own_points = pltpu.make_async_copy(points_ref, own_slot, chol_sem)
    chol_copy.wait()
    own_points.start()
    own_points.wait()

    row = lax.broadcasted_iota(jnp.int32, (TILE, TILE), 0)
    col = lax.broadcasted_iota(jnp.int32, (TILE, TILE), 1)

    share = tiles // 2
    first = core * share

    def own_block(b):
        at = pl.multiple_of((first + b) * TILE, TILE)
        return chol[pl.ds(at, TILE), pl.ds(at, TILE)]

    inverted = [jnp.where(row == col, 1.0 / own_block(b), 0.0) for b in range(share)]
    size = 1
    while size < TILE:
        below = (row // size == col // size + 1) & (row // (2 * size) == col // (2 * size))
        for b in range(share):
            off = jnp.where(below, own_block(b), 0.0)
            if size == 1:
                on_row = jnp.sum(inverted[b], axis=1, keepdims=True)
                on_col = jnp.sum(inverted[b], axis=0, keepdims=True)
                change = on_row * off * on_col
            else:
                change = dot_nn(dot_nn(inverted[b], off, HIGH), inverted[b], HIGH)
            inverted[b] = inverted[b] - change
        size *= 2
    for b in range(share):
        inverse[first + b] = inverted[b]

    wait_all(lambda to: rs_send.at[to], rs_recv, rs_sems)
    ag[me] = jnp.sum(rs_recv[...], axis=0)
    send_all(lambda to: ag.at[me], ag, ag_sems)

    shares = inverse.at[pl.ds(first, share)]
    shared = remote(shares, shares, share_sems.at[0], share_sems.at[1], partner)
    shared.start()

    def pass_on(s, both):
        near = row_of(pos - s, 0)
        remote(points_ref, points.at[near], point_fwd.at[near], point_recv.at[near], right).wait_recv()
        if both:
            remote(points.at[near], points.at[near], point_fwd.at[near], point_recv.at[near], right).start()
        remote(points.at[near], points.at[near], point_side.at[near], point_recv.at[near], partner).start()
        if both:
            far = row_of(pos + s, 0)
            remote(points_ref, points.at[far], point_fwd.at[far], point_recv.at[far], left).wait_recv()
            remote(points.at[far], points.at[far], point_side.at[far], point_recv.at[far], partner).start()

            @pl.when(s < half - 1)
            def _():
                remote(points.at[far], points.at[far], point_fwd.at[far], point_recv.at[far], left).start()

    def build_lanes(s, both):
        def build(lane):
            def one(way, carry):
                owner = row_of(pos - s + 2 * s * way, lane)
                if lane == 1:
                    remote(points_ref, points.at[owner], point_side.at[owner], point_recv.at[owner], partner).wait_recv()
                if keep:
                    make_block(owner, owner)
                return carry

            lax.fori_loop(0, 2 if both else 1, one, 0)

        build(0)
        build(1)

    pass_on(1, True)
    build_lanes(1, True)
    remote(points_ref, points.at[partner], point_side.at[partner], point_recv.at[partner], partner).wait_recv()

    other = inverse.at[pl.ds(share - first, share)]
    remote(other, other, share_sems.at[0], share_sems.at[1], partner).wait_recv()
    for b in range(groups):
        upper, lower = inverse[2 * b], inverse[2 * b + 1]
        at, end = b * GROUP, (b + 1) * GROUP
        off = chol[at + TILE:end, at:at + TILE]
        change = dot_nn(dot_nn(lower, off, HIGH), upper, HIGH)
        zero = jnp.zeros_like(upper)
        whole = jnp.concatenate(
            [jnp.concatenate([upper, zero], axis=1), jnp.concatenate([-change, lower], axis=1)], axis=0
        )
        store_split(inverse_parts, (b,), whole)
        if b > 0:
            store_split(chol_parts, (slice(at, end), slice(0, at)), chol[at:end, :at])

    pass_on(2, True)
    wait_all(lambda to: ag.at[me], ag, ag_sems)
    for piece in range(n):
        h, j = piece // tiles, piece % tiles
        work[h * rows_per:(h + 1) * rows_per, j * TILE:(j + 1) * TILE] = ag[piece]
    pieces = [work[:, b * GROUP:(b + 1) * GROUP] for b in range(groups)]

    def block_parts(i, j):
        rows, cols = slice(i * GROUP, (i + 1) * GROUP), slice(j * GROUP, (j + 1) * GROUP)
        return [chol_parts[term, rows, cols] for term in range(3)]

    def inverse_of(b):
        return [inverse_parts[term, b] for term in range(3)]

    for b in range(groups):
        pieces[b] = dot_split(pieces[b], inverse_of(b), dot_nt)
        for i in range(b + 1, groups):
            pieces[i] = pieces[i] - dot_split(pieces[b], block_parts(i, b), dot_nt)
    for b in reversed(range(groups)):
        pieces[b] = dot_split(pieces[b], inverse_of(b), dot_nn)
        for j in reversed(range(b)):
            pieces[j] = pieces[j] - dot_split(pieces[b], block_parts(b, j), dot_nn)
    coeffs = jnp.concatenate(pieces, axis=1)

    ridge = ridge_ref[0]
    residual = residual_ref[...]
    precond = (residual - dot_split(coeffs, [cross_t.at[term][...] for term in range(3)], dot_nn)) / ridge
    inner_buf[me] = to_row(jnp.sum(precond * residual, axis=1, keepdims=True), TILE)
    send_all(lambda to: inner_buf.at[me], inner_buf, inner_sems)

    pass_on(3, True)
    if keep:
        make_block(partner, partner)
    build_lanes(2, True)
    wait_all(lambda to: inner_buf.at[me], inner_buf, inner_sems)
    inner_row = jnp.sum(inner_buf[...], axis=0)
    inner_out[...] = inner_row[:, :outs]
    inner = to_column(inner_row)
    direction_new = precond + (inner / to_column(rz_ref[...])) * direction_ref[...]
    direction_out[...] = direction_new
    dirs[me] = direction_new.astype(jnp.bfloat16)
    send_all(lambda to: dirs.at[me], dirs, dir_sems)

    if keep:
        make_block(me, me)
    build_lanes(3, True)

    def later(s, carry):
        pass_on(s, True)
        build_lanes(s, True)
        return carry

    lax.fori_loop(4, half, later, 0)
    pass_on(half, False)
    build_lanes(half, False)

    def image_part(owner, slot):
        if not keep:
            make_block(owner, slot)
        proj[...] += dot_nn(dirs[owner], kernel_store[slot])

    proj[...] = jnp.zeros_like(proj)
    image_part(me, me if keep else 0)

    def gather_image(to):
        remote(dirs.at[me], dirs.at[to], dir_sems.at[0, to], dir_sems.at[1, to], to).wait_recv()
        image_part(to, to if keep else 0)

    others(gather_image)

    direction_new = direction_out[...]
    image = proj[...] + ridge * direction_new
    image_out[...] = image
    curv_buf[me] = to_row(jnp.sum(direction_new * image, axis=1, keepdims=True), TILE)
    send_all(lambda to: curv_buf.at[me], curv_buf, curv_sems)

    drain(lambda to: rs_send.at[to], rs_recv, rs_sems)
    drain(lambda to: ag.at[me], ag, ag_sems)
    drain(lambda to: inner_buf.at[me], inner_buf, inner_sems)
    drain(lambda to: dirs.at[me], dirs, dir_sems)
    shared.wait_send()
    first_right.wait_send()
    first_left.wait_send()
    first_side.wait_send()

    def relay_drain(s, both):
        near = row_of(pos - s, 0)
        remote(points.at[near], points.at[near], point_side.at[near], point_recv.at[near], partner).wait_send()
        if both:
            remote(points.at[near], points.at[near], point_fwd.at[near], point_recv.at[near], right).wait_send()
            far = row_of(pos + s, 0)
            remote(points.at[far], points.at[far], point_side.at[far], point_recv.at[far], partner).wait_send()

            @pl.when(s < half - 1)
            def _():
                remote(points.at[far], points.at[far], point_fwd.at[far], point_recv.at[far], left).wait_send()

    lax.fori_loop(1, half, lambda s, carry: (relay_drain(s, True), carry)[1], 0)
    relay_drain(half, False)

    wait_all(lambda to: curv_buf.at[me], curv_buf, curv_sems)
    alpha_out[...] = inner_out[...] / jnp.sum(curv_buf[...], axis=0)[:, :outs]
    drain(lambda to: curv_buf.at[me], curv_buf, curv_sems)


def finish(
    image_ref,
    direction_ref,
    inner_ref,
    alpha_ref,
    solution_ref,
    residual_ref,
    solution_out,
    residual_out,
    direction_out,
    inner_out,
):
    alpha = to_column(alpha_ref[...])
    direction = direction_ref[...]
    solution_out[...] = solution_ref[...] + alpha * direction
    residual_out[...] = residual_ref[...] - alpha * image_ref[...]
    direction_out[...] = direction
    inner_out[...] = inner_ref[...]


def solution(mesh):
    n = mesh.shape["rows"]

    def local(points, landmarks, chol, ridge, solution, residual, direction, rz_prev):
        feat, own = points.shape
        land = landmarks.shape[1]
        outs = residual.shape[0]
        keep = n <= STORED_BLOCKS
        piece = outs * land // (TILE * n)
        f32, bf16 = jnp.float32, jnp.bfloat16
        vmem = pl.BlockSpec(memory_space=pltpu.VMEM)
        wide = jax.ShapeDtypeStruct((outs, own), f32)
        thin = jax.ShapeDtypeStruct((1, outs), f32)
        dma = pltpu.SemaphoreType.DMA
        results = pl.pallas_call(
            functools.partial(kernel, n, keep),
            out_shape=(wide, wide, thin, thin),
            in_specs=[
                vmem,
                vmem,
                pl.BlockSpec(memory_space=pl.ANY),
                pl.BlockSpec(memory_space=pltpu.SMEM),
                vmem,
                vmem,
                vmem,
            ],
            out_specs=(vmem,) * 4,
            scratch_shapes=[
                pltpu.VMEM((land, land), f32),
                pltpu.VMEM((3, land, land), bf16),
                pltpu.VMEM((3, land // GROUP, GROUP, GROUP), bf16),
                pltpu.VMEM((land // TILE, TILE, TILE), f32),
                pltpu.VMEM((n, feat, own), bf16),
                pltpu.VMEM((feat + 16, own), bf16),
                pltpu.VMEM((feat + 16, own), bf16),
                pltpu.VMEM((3, land, own), bf16),
                pltpu.VMEM((n if keep else 1, own, own), bf16),
                pltpu.VMEM((n, piece, TILE), f32),
                pltpu.VMEM((n, piece, TILE), f32),
                pltpu.VMEM((n, piece, TILE), f32),
                pltpu.VMEM((outs, land), f32),
                pltpu.VMEM((outs, land), f32),
                pltpu.VMEM((n, 1, TILE), f32),
                pltpu.VMEM((n, outs, own), bf16),
                pltpu.VMEM((n, 1, TILE), f32),
                dma,
                dma((2, n)),
                dma((2, n)),
                dma((2, n)),
                dma((2, n)),
                dma((2, n)),
                dma((n,)),
                dma((n,)),
                dma((n,)),
                dma,
                dma((2,)),
            ],
            compiler_params=pltpu.CompilerParams(
                collective_id=0, has_side_effects=True, vmem_limit_bytes=62 * 1024 * 1024
            ),
            name="cg_step",
        )(points, landmarks, chol, ridge, residual, direction, rz_prev.reshape(1, outs))
        results = pl.pallas_call(
            finish,
            out_shape=(wide, wide, wide, thin),
            in_specs=[vmem] * 6,
            out_specs=(vmem,) * 4,
            name="finish",
        )(*results, solution, residual)
        return (results[0], results[1], results[2], results[3].reshape(outs))

    wide_spec = P(None, ("groups", "rows"))
    in_specs = (
        wide_spec,
        P(None, "groups"),
        P("groups", None),
        P("groups"),
        wide_spec,
        wide_spec,
        wide_spec,
        P("groups"),
    )
    out_specs = (wide_spec, wide_spec, wide_spec, P("groups"))
    return jax.shard_map(local, mesh=mesh, in_specs=in_specs, out_specs=out_specs, check_vma=False)
```
